32 devices in a mesh: band: 4 (over y, core), shard: 8 (over z, x).
Axes of the slice: x: 2, y: 2, z: 4, core: 2. Of those that a mesh axis runs over, the one named last changes fastest.
Arguments:
- activations: bfloat16 [512, 2304], P('shard'), may hold values from -6 to 6
- encoder: bfloat16 [2304, 16384], P(None, ('band', 'shard')), may hold values from -0.125 to 0.125
- encoder_bias: float32 [16384], P(('band', 'shard')), may hold values from -1 to -0.25
- decoder: bfloat16 [16384, 2304], P(('band', 'shard')), may hold values from -0.125 to 0.125
Outputs:
- losses: float32 [4], replicated
- encoder_grad: bfloat16 [2304, 16384], P(None, ('band', 'shard'))
- decoder_grad: bfloat16 [16384, 2304], P(('band', 'shard'))
The draws below stay inside these ranges and needn't reach their ends.
All inputs are finite; a program needn't handle non-finite values.
Results may differ from the reference program's by a relative error of at most 0.006.
Values may be sent and summed in bfloat16 or wider, within the bound.
A program may use at most 128 MiB of HBM per device.

```python
import jax
import jax.numpy as jnp
from jax import lax

D = 2304
LATENTS = 16384
ROWS = 512
N_BAND = 4


def block_levels(key, extent, cuts, least, top_value):
    factor_of = 1.0
    for position, shards_of in cuts:
        steps = jax.random.uniform(jax.random.fold_in(jax.random.fold_in(key, 6), position), (shards_of,), jnp.float32, least / len(cuts), top_value / len(cuts))
        factor_of = factor_of * jnp.repeat(jnp.exp(steps), extent[position] // shards_of).reshape((-1,) + (1,) * (len(extent) - 1 - position))
    return factor_of


def bell_draw(key, shape, scale, most, pieces=(), held_as=jnp.bfloat16):
    loudness = block_levels(key, shape, pieces, -0.22, 0.18) if pieces else 1.0
    array = jax.random.normal(key, shape, jnp.float32) * scale * loudness
    return jnp.minimum(jnp.maximum(array, -most), most).astype(held_as)


def setup_inputs(seed: int = 0) -> dict:
    splits = jax.random.split(jax.random.key(seed), 5)
    activations = bell_draw(splits[0], (ROWS, D), 1.0, 6.0, ((0, 8),))
    encoder = bell_draw(splits[1], (D, LATENTS), D ** -0.5, 0.125, ((1, 32),))
    encoder_bias = jnp.clip(-1.0 + 0.75 * jax.random.uniform(splits[2], (LATENTS,), jnp.float32) ** block_levels(splits[2], (LATENTS,), ((0, 32),), -0.2, 0.2), -1.0, -0.25)
    decoder = bell_draw(splits[3], (LATENTS, D), D ** -0.5, 0.125, ((0, 32),))
    return {"activations": activations, "encoder": encoder, "encoder_bias": encoder_bias, "decoder": decoder}


def reference(activations, encoder, encoder_bias, decoder):
    band_count = N_BAND
    width = LATENTS // band_count
    enc_bands = encoder.reshape(D, band_count, width).transpose(1, 0, 2)
    bias_bands = encoder_bias.reshape(band_count, width)
    dec_bands = decoder.reshape(band_count, width, D)

    def forward(items):
        weight, bias, back = items
        preact = jnp.dot(activations, weight, preferred_element_type=jnp.float32) + bias
        linear = jnp.maximum(preact, 0.0)
        active = (linear * linear).astype(jnp.bfloat16)
        part = jnp.dot(active, back, preferred_element_type=jnp.float32)
        return active, linear, part

    active, linears, parts = lax.map(forward, (enc_bands, bias_bands, dec_bands))
    recon = jnp.cumsum(parts, axis=0)
    errors = activations.astype(jnp.float32)[None] - recon
    losses = jnp.sum(errors * errors, axis=(1, 2)) / (ROWS * D)
    suffix = jnp.flip(jnp.cumsum(jnp.flip(errors, 0), axis=0), 0)
    upstream = (-suffix / band_count).astype(jnp.bfloat16)

    def backward(items):
        acted, linear, back, grad = items
        act_grads = jnp.dot(grad, back.T, preferred_element_type=jnp.float32)
        pre_grads = (2.0 * linear * act_grads).astype(jnp.bfloat16)
        enc_grad = jnp.dot(activations.T, pre_grads, preferred_element_type=jnp.float32).astype(jnp.bfloat16)
        dec_grad = jnp.dot(acted.T, grad, preferred_element_type=jnp.float32).astype(jnp.bfloat16)
        return enc_grad, dec_grad

    enc_grads, dec_grads = lax.map(backward, (active, linears, dec_bands, upstream))
    encoder_grad = enc_grads.transpose(1, 0, 2).reshape(D, LATENTS)
    decoder_grad = dec_grads.reshape(LATENTS, D)
    return (losses, encoder_grad, decoder_grad)
```

```python
import functools

import jax
import jax.numpy as jnp
from jax import lax
from jax.experimental import pallas as pl
from jax.experimental.pallas import tpu as pltpu
from jax.sharding import PartitionSpec as P

MESH = pl.DeviceIdType.MESH
CHUNKS = 2
F32 = jnp.float32
BF16 = jnp.bfloat16


def factors(count):
    outer = next(a for a in range(1, count + 1) if count % a == 0 and a * a >= count)
    return outer, count // outer


def ring_position(index, outer, inner):
    z, x = index // inner, index % inner
    return x * outer + z + (x % 2) * (outer - 1 - 2 * z)


def ring_index(position, outer, inner):
    x, r = position // outer, position % outer
    z = r + (x % 2) * (outer - 1 - 2 * r)
    return z * inner + x


def tile_of(extent, most):
    return next(t for t in range(most, 0, -128) if extent % t == 0)


def kernel(
    n, nb,
    act_ref, act3_ref, enc_hbm, bias_ref, dec_hbm,
    gath, ups, active, pregr, loss_ref,
    enc, dec, linear, part, sendb, recvb, xsend, xrecv, usend, urecv, loss_acc, loss1s, loss1, loss2s, loss2,
    load_sem,
    ag_s, ag_r, pt_s, pt_r, rs_s, rs_r, bx_s, bx_r, bu_s, bu_r, l1_s, l1_r, l2_s, l2_r, ug_s, ug_r,
):
    rows, width = act_ref.shape
    half = rows // 2
    chunk = rows // CHUNKS
    thin = rows // nb
    latents = enc.shape[1]
    fwd, bwd = n // 2, n // 2 - 1
    outer, inner = factors(n)
    band = lax.axis_index("band")
    shard = lax.axis_index("shard")
    core = band % 2
    sign = 1 - 2 * core
    place = ring_position(shard, outer, inner)
    nxt = {"shard": ring_index((place + n + sign) % n, outer, inner)}
    prv = {"shard": ring_index((place + n - sign) % n, outer, inner)}
    mate = {"band": band + sign}
    ours = pl.multiple_of(core * half, half)

    load_enc = pltpu.make_async_copy(enc_hbm, enc, load_sem.at[0])
    load_dec = pltpu.make_async_copy(dec_hbm, dec, load_sem.at[1])
    load_enc.start()
    load_dec.start()

    barrier = pltpu.get_barrier_semaphore()
    for step in range(1, n):
        pl.semaphore_signal(barrier, inc=1, device_id={"shard": (shard + step) % n}, device_id_type=MESH)
    for step in range(1, nb):
        pl.semaphore_signal(barrier, inc=1, device_id={"band": (band + step) % nb}, device_id_type=MESH)
    pl.semaphore_wait(barrier, n - 1 + nb - 1)

    started = []

    def remote(src, dst, send, recv, device):
        return pltpu.make_async_remote_copy(
            src_ref=src, dst_ref=dst, send_sem=send, recv_sem=recv, device_id=device, device_id_type=MESH
        )

    def go(copy):
        copy.start()
        started.append(copy)
        return copy

    def held(slot):
        return gath.at[pl.ds(pl.multiple_of(slot * rows + ours, half), half), :]

    mine = act_ref.at[pl.ds(ours, half), :]

    def ag_copy(way, t):
        if way == 0:
            src = mine if t == 1 else held(n - t + 1)
            return remote(src, held(n - t), ag_s.at[0, t], ag_r.at[0, t], nxt)
        src = mine if t == 1 else held(t - 1)
        return remote(src, held(t), ag_s.at[1, t], ag_r.at[1, t], prv)

    def mate_copy(slot):
        there = n - slot
        return remote(held(slot), held(there), pt_s.at[slot], pt_r.at[there], mate)

    def preact(group):
        span = pl.ds(group * 2 * rows, 2 * rows)
        value = jnp.dot(gath[span, :], enc[...], preferred_element_type=F32) + bias_ref[...]
        value = jnp.maximum(value, 0.0)
        linear[span, :] = value
        active[span, :] = (value * value).astype(BF16)

    def ready(slot):
        return slot if slot <= bwd else n - slot

    ag = {(0, 1): go(ag_copy(0, 1)), (1, 1): go(ag_copy(1, 1))}
    gath[pl.ds(0, rows), :] = act_ref[...]
    mates = {}
    for t in range(1, fwd + 1):
        ag[0, t].wait_recv()
        if t < fwd:
            ag[0, t + 1] = go(ag_copy(0, t + 1))
        mates[n - t] = go(mate_copy(n - t))
        if t <= bwd:
            ag[1, t].wait_recv()
            if t < bwd:
                ag[1, t + 1] = go(ag_copy(1, t + 1))
            mates[t] = go(mate_copy(t))
        for group in range(n // 2):
            pair = (2 * group, 2 * group + 1)
            if max(ready(s) for s in pair) == t:
                for s in pair:
                    if s:
                        remote(held(s), held(s), pt_s.at[n - s], pt_r.at[s], mate).wait_recv()
                if t == 1:
                    load_enc.wait()
                preact(group)
    load_dec.wait()

    tile = tile_of(width, 768)

    def decode(group):
        span = pl.ds(group * 2 * rows, 2 * rows)

        def body(i, carry):
            cols = pl.ds(pl.multiple_of(i * tile, tile), tile)
            part[span, cols] = jnp.dot(active[span, :], dec[:, cols], preferred_element_type=F32)
            return carry

        lax.fori_loop(0, width // tile, body, 0)

    def need(slot):
        return n if slot == 0 else (fwd - slot + 1 if slot <= fwd else slot - fwd)

    def rs_copy(way, t, c):
        slot = fwd - t + 1 if way == 0 else fwd + t
        there = slot - 1 if way == 0 else (slot + 1 if slot + 1 < n else fwd)
        span = pl.ds(c * chunk, chunk)
        return remote(
            sendb.at[slot, span, :], recvb.at[there, span, :], rs_s.at[way, t, c], rs_r.at[way, t, c],
            nxt if way == 0 else prv,
        )

    order = sorted(range(n // 2), key=lambda g: min(need(2 * g), need(2 * g + 1)))
    first = [g for g in order if min(need(2 * g), need(2 * g + 1)) == 1]
    for group in first:
        decode(group)
    rs = {}
    for t in range(1, fwd + 1):
        for c in range(CHUNKS):
            for way in (0, 1):
                if way == 1 and t > bwd:
                    continue
                slot = fwd - t + 1 if way == 0 else fwd + t
                span = pl.ds(c * chunk, chunk)
                value = part[pl.ds(slot * rows + c * chunk, chunk), :]
                if t > 1:
                    rs[way, t - 1, c].wait_recv()
                    value = value + recvb[slot, span, :].astype(F32)
                sendb[slot, span, :] = value.astype(BF16)
                rs[way, t, c] = go(rs_copy(way, t, c))
        if t == 1:
            for group in order:
                if group not in first:
                    decode(group)
    for c in range(CHUNKS):
        span = pl.ds(c * chunk, chunk)
        rs[1, bwd, c].wait_recv()
        rs[0, fwd, c].wait_recv()
        part[span, :] = part[span, :] + recvb[0, span, :].astype(F32) + recvb[fwd, span, :].astype(F32)

    for k in range(nb):
        xsend[k] = part[pl.ds(k * thin, thin), :].astype(BF16)
    bx = [
        go(remote(xsend.at[(band + i) % nb], xrecv.at[band], bx_s.at[i], bx_r.at[i], {"band": (band + i) % nb}))
        for i in range(1, nb)
    ]
    xrecv[band] = xsend[band]
    for copy in bx:
        copy.wait_recv()

    step_cols = tile_of(width, 256)

    def errors(i, carry):
        cols = pl.ds(pl.multiple_of(i * step_cols, step_cols), step_cols)
        left = act3_ref[band, :, cols].astype(F32)
        all_errors = []
        for k in range(nb):
            left = left - xrecv[k, :, cols].astype(F32)
            all_errors.append(left)
            loss_acc[pl.ds(k, 1), cols] = jnp.sum(left * left, axis=0, keepdims=True)
        total = jnp.zeros_like(left)
        for k in reversed(range(nb)):
            total = total + all_errors[k]
            usend[k, :, cols] = (-total / nb).astype(BF16)
        return carry

    lax.fori_loop(0, width // step_cols, errors, 0)
    bu = [
        go(remote(usend.at[(band + i) % nb], urecv.at[band], bu_s.at[i], bu_r.at[i], {"band": (band + i) % nb}))
        for i in range(1, nb)
    ]
    urecv[band] = usend[band]
    loss1s[...] = jnp.broadcast_to(jnp.sum(loss_acc[...], axis=1, keepdims=True), loss1s.shape)
    l1 = [
        go(remote(loss1s, loss1.at[i], l1_s.at[i], l1_r.at[i], {"band": (band + i) % nb}))
        for i in range(1, nb)
    ]
    for copy in bu:
        copy.wait_recv()
    if thin % 16 == 0:
        for k in range(nb):
            ups[pl.ds(k * thin, thin), :] = urecv[k]
    else:
        ups[pl.ds(0, rows), :] = jnp.concatenate([urecv[k].astype(F32) for k in range(nb)], axis=0).astype(BF16)

    def ug_copy(way, t, c):
        if way == 0:
            slot, there, device = (n - t + 1) % n, n - t, nxt
        else:
            slot, there, device = t - 1, t, prv
        return remote(
            ups.at[pl.ds(slot * rows + c * chunk, chunk), :], ups.at[pl.ds(there * rows + c * chunk, chunk), :],
            ug_s.at[way, t, c], ug_r.at[way, t, c], device,
        )

    ug = {}
    for c in range(CHUNKS):
        for way in (0, 1):
            ug[way, 1, c] = go(ug_copy(way, 1, c))

    for copy in l1:
        copy.wait_recv()
    total = loss1s[...]
    for i in range(1, nb):
        total = total + loss1[i]
    loss2s[...] = total
    l2 = [
        go(remote(loss2s, loss2.at[i], l2_s.at[i], l2_r.at[i], {"shard": (shard + i) % n}))
        for i in range(1, n)
    ]

    def backward(group):
        span = pl.ds(group * 2 * rows, 2 * rows)
        grads = lax.dot_general(ups[span, :], dec[...], (((1,), (1,)), ((), ())), preferred_element_type=F32)
        pregr[span, :] = (2.0 * linear[span, :] * grads).astype(BF16)

    for t in range(1, fwd + 1):
        for c in range(CHUNKS):
            for way in (0, 1):
                last = fwd if way == 0 else bwd
                if t > last:
                    continue
                ug[way, t, c].wait_recv()
                if t < last:
                    ug[way, t + 1, c] = go(ug_copy(way, t + 1, c))
        for group in range(n // 2):
            if max(ready(2 * group), ready(2 * group + 1)) == t:
                backward(group)

    for copy in l2:
        copy.wait_recv()
    total = loss2s[...]
    for i in range(1, n):
        total = total + loss2[i]
    loss_ref[...] = total
    for copy in started:
        copy.wait_send()


def on_device(n, nb, activations, encoder, encoder_bias, decoder):
    rows, width = activations.shape
    latents = encoder.shape[1]
    every = n * rows
    thin = rows // nb
    sem = pltpu.SemaphoreType.DMA
    vmem = pl.BlockSpec(memory_space=pltpu.VMEM)
    hbm = pl.BlockSpec(memory_space=pl.ANY)
    steps = n // 2 + 1
    gathered, upstream, active, pre_grads, losses = pl.pallas_call(
        functools.partial(kernel, n, nb),
        out_shape=(
            jax.ShapeDtypeStruct((every, width), BF16),
            jax.ShapeDtypeStruct((every, width), BF16),
            jax.ShapeDtypeStruct((every, latents), BF16),
            jax.ShapeDtypeStruct((every, latents), BF16),
            jax.ShapeDtypeStruct((nb, 128), F32),
        ),
        in_specs=[vmem, vmem, hbm, vmem, hbm],
        out_specs=[vmem] * 5,
        scratch_shapes=[
            pltpu.VMEM((width, latents), BF16),
            pltpu.VMEM((latents, width), BF16),
            pltpu.VMEM((every, latents), F32),
            pltpu.VMEM((every, width), F32),
            pltpu.VMEM((n, rows, width), BF16),
            pltpu.VMEM((n, rows, width), BF16),
            pltpu.VMEM((nb, thin, width), BF16),
            pltpu.VMEM((nb, thin, width), BF16),
            pltpu.VMEM((nb, thin, width), BF16),
            pltpu.VMEM((nb, thin, width), BF16),
            pltpu.VMEM((nb, width), F32),
            pltpu.VMEM((nb, 128), F32),
            pltpu.VMEM((nb, nb, 128), F32),
            pltpu.VMEM((nb, 128), F32),
            pltpu.VMEM((n, nb, 128), F32),
            sem((2,)),
            sem((2, steps)), sem((2, steps)),
            sem((n,)), sem((n,)),
            sem((2, steps, CHUNKS)), sem((2, steps, CHUNKS)),
            sem((nb,)), sem((nb,)),
            sem((nb,)), sem((nb,)),
            sem((nb,)), sem((nb,)),
            sem((n,)), sem((n,)),
            sem((2, steps, CHUNKS)), sem((2, steps, CHUNKS)),
        ],
        compiler_params=pltpu.CompilerParams(
            collective_id=0, has_side_effects=True, vmem_limit_bytes=60 * 1024 * 1024
        ),
    )(activations, activations.reshape(nb, thin, width), encoder, encoder_bias.reshape(1, latents), decoder)
    encoder_grad = jnp.einsum("rd,rl->dl", gathered, pre_grads, preferred_element_type=F32).astype(BF16)
    decoder_grad = jnp.einsum("rl,rd->ld", active, upstream, preferred_element_type=F32).astype(BF16)
    return losses[:, 0] / (every * width), encoder_grad, decoder_grad


def solution(mesh):
    n, nb = mesh.shape["shard"], mesh.shape["band"]
    return jax.shard_map(
        functools.partial(on_device, n, nb),
        mesh=mesh,
        in_specs=(
            P("shard", None),
            P(None, ("band", "shard")),
            P(("band", "shard")),
            P(("band", "shard"), None),
        ),
        out_specs=(P(), P(None, ("band", "shard")), P(("band", "shard"), None)),
        check_vma=False,
    )
```

```python
import functools

import jax
import jax.numpy as jnp
from jax import lax
from jax.experimental import pallas as pl
from jax.experimental.pallas import tpu as pltpu
from jax.sharding import PartitionSpec as P

MESH = pl.DeviceIdType.MESH
PARTS = 2
LAG = 0
F32 = jnp.float32
BF16 = jnp.bfloat16


def factors(count):
    outer = next(a for a in range(1, count + 1) if count % a == 0 and a * a >= count)
    return outer, count // outer


def ring_position(index, outer, inner):
    z, x = index // inner, index % inner
    return x * outer + z + (x % 2) * (outer - 1 - 2 * z)


def ring_index(position, outer, inner):
    x, r = position // outer, position % outer
    z = r + (x % 2) * (outer - 1 - 2 * r)
    return z * inner + x


def tile_of(extent, most):
    return next(t for t in range(most, 0, -128) if extent % t == 0)


def kernel(
    n, nb,
    act_ref, act3_ref, enc_hbm, bias_ref, dec_hbm,
    gath_t_hbm, ups_hbm, active_hbm, pregr_hbm, loss_ref,
    gath, gath_t, ups, active, pregr,
    enc, dec, linear, part, sendb, recvb, xsend, xrecv, usend, urecv, loss_acc, loss1s, loss1, loss2s, loss2,
    load_sem, out_sem,
    ag_s, ag_r, pt_s, pt_r, rs_s, rs_r, bx_s, bx_r, bu_s, bu_r, l1_s, l1_r, l2_s, l2_r, ug_s, ug_r,
):
    width = act_ref.shape[1]
    rows = act_ref.shape[0] // PARTS
    half = rows // 2
    thin = rows // nb
    fwd, bwd = n // 2, n // 2 - 1
    outer, inner = factors(n)
    band = lax.axis_index("band")
    shard = lax.axis_index("shard")
    core = band % 2
    sign = 1 - 2 * core
    place = ring_position(shard, outer, inner)
    nxt = {"shard": ring_index((place + n + sign) % n, outer, inner)}
    prv = {"shard": ring_index((place + n - sign) % n, outer, inner)}
    mate = {"band": band + sign}

    load_enc = pltpu.make_async_copy(enc_hbm, enc, load_sem.at[0])
    load_dec = pltpu.make_async_copy(dec_hbm, dec, load_sem.at[1])
    load_enc.start()
    load_dec.start()

    barrier = pltpu.get_barrier_semaphore()
    for device in [nxt, prv] + [{"band": (band + i) % nb} for i in range(1, nb)]:
        pl.semaphore_signal(barrier, inc=1, device_id=device, device_id_type=MESH)
    pl.semaphore_wait(barrier, nb + 1)

    started = []
    written = []

    def remote(src, dst, send, recv, device):
        return pltpu.make_async_remote_copy(
            src_ref=src, dst_ref=dst, send_sem=send, recv_sem=recv, device_id=device, device_id_type=MESH
        )

    def go(copy):
        copy.start()
        started.append(copy)
        return copy

    def write(src, dst, index):
        copy = pltpu.make_async_copy(src, dst, out_sem.at[index])
        copy.start()
        written.append(copy)

    tile = tile_of(width, 768)
    step_cols = tile_of(width, 256)
    l1 = []

    def batch(m):
        base = m * n * rows

        def at(slot):
            return pl.ds(base + slot * rows, rows)

        def group_span(upper):
            return pl.ds(base + upper * fwd * rows, fwd * rows)

        def held(slot):
            start = pl.multiple_of(base + slot * rows + core * half, half)
            return gath.at[pl.ds(start, half), :]

        mine = act_ref.at[pl.ds(pl.multiple_of(m * rows + core * half, half), half), :]

        def ag_copy(way, t):
            if way == 0:
                src = mine if t == 1 else held(n - t + 1)
                return remote(src, held(n - t), ag_s.at[m, 0, t], ag_r.at[m, 0, t], nxt)
            src = mine if t == 1 else held(t - 1)
            return remote(src, held(t), ag_s.at[m, 1, t], ag_r.at[m, 1, t], prv)

        def mate_copy(slot):
            there = n - slot
            return remote(held(slot), held(there), pt_s.at[m, slot], pt_r.at[m, there], mate)

        def mate_wait(s):
            remote(held(s), held(s), pt_s.at[m, n - s], pt_r.at[m, s], mate).wait_recv()

        def preact(upper):
            span = group_span(upper)
            value = jnp.dot(gath[span, :], enc[...], preferred_element_type=F32) + bias_ref[...]
            value = jnp.maximum(value, 0.0)
            linear[span, :] = value
            active[span, :] = (value * value).astype(BF16)
            write(active.at[span, :], active_hbm.at[span, :], (0, m, upper))

        def transpose(upper):
            span = group_span(upper)
            gath_t[:, span] = gath[span, :].T
            write(gath_t.at[:, span], gath_t_hbm.at[:, span], (1, m, upper))

        def decode(upper):
            span = group_span(upper)

            def body(i, carry):
                cols = pl.ds(pl.multiple_of(i * tile, tile), tile)
                part[span, cols] = jnp.dot(active[span, :], dec[:, cols], preferred_element_type=F32)
                return carry

            lax.fori_loop(0, width // tile, body, 0)

        ag = {(0, 1): go(ag_copy(0, 1)), (1, 1): go(ag_copy(1, 1))}
        gath[at(0), :] = act_ref[pl.ds(m * rows, rows), :]
        yield
        for t in range(1, fwd + 1):
            ag[0, t].wait_recv()
            if t < fwd:
                ag[0, t + 1] = go(ag_copy(0, t + 1))
            go(mate_copy(n - t))
            if t <= bwd:
                ag[1, t].wait_recv()
                if t < bwd:
                    ag[1, t + 1] = go(ag_copy(1, t + 1))
                go(mate_copy(t))
            if t < fwd:
                yield
            if t == bwd:
                for s in range(1, fwd):
                    mate_wait(s)
                if m == 0:
                    load_enc.wait()
                preact(0)
        for s in range(fwd, n):
            mate_wait(s)
        if bwd == 0:
            if m == 0:
                load_enc.wait()
            preact(0)
        preact(1)
        if m == 0:
            load_dec.wait()
        decode(1)

        rs = {}

        def rs_copy(way, t):
            slot = fwd - t + 1 if way == 0 else fwd + t
            there = slot - 1 if way == 0 else (slot + 1 if slot + 1 < n else fwd)
            return remote(
                sendb.at[m * n + slot], recvb.at[m * n + there], rs_s.at[m, way, t], rs_r.at[m, way, t],
                nxt if way == 0 else prv,
            )

        for t in range(1, fwd + 1):
            for way in (0, 1):
                if way == 1 and t > bwd:
                    continue
                slot = fwd - t + 1 if way == 0 else fwd + t
                value = part[at(slot), :]
                if t > 1:
                    rs[way, t - 1].wait_recv()
                    value = value + recvb[m * n + slot].astype(F32)
                sendb[m * n + slot] = value.astype(BF16)
                rs[way, t] = go(rs_copy(way, t))
            yield
            if t == 1:
                decode(0)
        if bwd:
            rs[1, bwd].wait_recv()
        rs[0, fwd].wait_recv()
        value = part[at(0), :] + recvb[m * n].astype(F32)
        if bwd:
            value = value + recvb[m * n + fwd].astype(F32)
        part[at(0), :] = value
        for k in range(nb):
            xsend[m * nb + k] = part[pl.ds(base + k * thin, thin), :].astype(BF16)
        bx = [
            go(remote(
                xsend.at[m * nb + (band + i) % nb], xrecv.at[m * nb + band], bx_s.at[m, i], bx_r.at[m, i],
                {"band": (band + i) % nb},
            ))
            for i in range(1, nb)
        ]
        xrecv[m * nb + band] = xsend[m * nb + band]
        transpose(0)
        yield
        for copy in bx:
            copy.wait_recv()

        def errors(i, carry):
            cols = pl.ds(pl.multiple_of(i * step_cols, step_cols), step_cols)
            left = act3_ref[m * nb + band, :, cols].astype(F32)
            all_errors = []
            for k in range(nb):
                left = left - xrecv[m * nb + k, :, cols].astype(F32)
                all_errors.append(left)
                loss_acc[pl.ds(m * nb + k, 1), cols] = jnp.sum(left * left, axis=0, keepdims=True)
            total = jnp.zeros_like(left)
            for k in reversed(range(nb)):
                total = total + all_errors[k]
                usend[m * nb + k, :, cols] = (-total / nb).astype(BF16)
            return carry

        lax.fori_loop(0, width // step_cols, errors, 0)
        bu = [
            go(remote(
                usend.at[m * nb + (band + i) % nb], urecv.at[m * nb + band], bu_s.at[m, i], bu_r.at[m, i],
                {"band": (band + i) % nb},
            ))
            for i in range(1, nb)
        ]
        urecv[m * nb + band] = usend[m * nb + band]
        if m == PARTS - 1:
            sums = loss_acc[pl.ds(0, nb), :]
            for other in range(1, PARTS):
                sums = sums + loss_acc[pl.ds(other * nb, nb), :]
            loss1s[...] = jnp.broadcast_to(jnp.sum(sums, axis=1, keepdims=True), loss1s.shape)
            for i in range(1, nb):
                l1.append(go(remote(
                    loss1s, loss1.at[i], l1_s.at[i], l1_r.at[i], {"band": (band + i) % nb}
                )))
        transpose(1)
        yield
        for copy in bu:
            copy.wait_recv()
        ups[at(0), :] = jnp.concatenate([urecv[m * nb + k].astype(F32) for k in range(nb)], axis=0).astype(BF16)

        def ug_copy(way, t):
            if way == 0:
                slot, there, device = (n - t + 1) % n, n - t, nxt
            else:
                slot, there, device = t - 1, t, prv
            return remote(ups.at[at(slot), :], ups.at[at(there), :], ug_s.at[m, way, t], ug_r.at[m, way, t], device)

        def backward(upper):
            span = group_span(upper)
            grads = lax.dot_general(ups[span, :], dec[...], (((1,), (1,)), ((), ())), preferred_element_type=F32)
            pregr[span, :] = (2.0 * linear[span, :] * grads).astype(BF16)
            write(pregr.at[span, :], pregr_hbm.at[span, :], (3, m, upper))

        ug = {}
        for way in (0, 1):
            if way == 0 or bwd:
                ug[way, 1] = go(ug_copy(way, 1))
        yield
        for t in range(1, fwd + 1):
            for way in (0, 1):
                last = fwd if way == 0 else bwd
                if t > last:
                    continue
                ug[way, t].wait_recv()
                if t < last:
                    ug[way, t + 1] = go(ug_copy(way, t + 1))
            if t == fwd:
                write(ups.at[group_span(1), :], ups_hbm.at[group_span(1), :], (2, m, 1))
            yield
            if t == max(bwd, 1):
                write(ups.at[group_span(0), :], ups_hbm.at[group_span(0), :], (2, m, 0))
                backward(0)
        backward(1)

    work = [batch(m) for m in range(PARTS)]
    done = set()
    turn = 0
    while len(done) < PARTS:
        for m in range(PARTS):
            if m in done or turn < m * LAG:
                continue
            if next(work[m], "end") == "end":
                done.add(m)
        turn += 1
        if not len(done) and l1 and turn == n + 4 + (PARTS - 1) * LAG:
            for copy in l1:
                copy.wait_recv()
            total = loss1s[...]
            for i in range(1, nb):
                total = total + loss1[i]
            loss2s[...] = total
            l2 = [
                go(remote(loss2s, loss2.at[i], l2_s.at[i], l2_r.at[i], {"shard": (shard + i) % n}))
                for i in range(1, n)
            ]
    for copy in l2:
        copy.wait_recv()
    total = loss2s[...]
    for i in range(1, n):
        total = total + loss2[i]
    for k in range(nb):
        loss_ref[k] = jnp.sum(total[k:k + 1, 0:1]) / (n * act_ref.shape[0] * width)
    for copy in started:
        copy.wait_send()
    for copy in written:
        copy.wait()


def on_device(n, nb, activations, encoder, encoder_bias, decoder):
    local, width = activations.shape
    latents = encoder.shape[1]
    rows = local // PARTS
    every = n * local
    thin = rows // nb
    sem = pltpu.SemaphoreType.DMA
    vmem = pl.BlockSpec(memory_space=pltpu.VMEM)
    hbm = pl.BlockSpec(memory_space=pl.ANY)
    steps = n // 2 + 1
    gathered_t, upstream, active, pre_grads, losses = pl.pallas_call(
        functools.partial(kernel, n, nb),
        out_shape=(
            jax.ShapeDtypeStruct((width, every), BF16),
            jax.ShapeDtypeStruct((every, width), BF16),
            jax.ShapeDtypeStruct((every, latents), BF16),
            jax.ShapeDtypeStruct((every, latents), BF16),
            jax.ShapeDtypeStruct((nb,), F32),
        ),
        in_specs=[vmem, vmem, hbm, vmem, hbm],
        out_specs=[hbm] * 4 + [pl.BlockSpec(memory_space=pltpu.SMEM)],
        scratch_shapes=[
            pltpu.VMEM((every, width), BF16),
            pltpu.VMEM((width, every), BF16),
            pltpu.VMEM((every, width), BF16),
            pltpu.VMEM((every, latents), BF16),
            pltpu.VMEM((every, latents), BF16),
            pltpu.VMEM((width, latents), BF16),
            pltpu.VMEM((latents, width), BF16),
            pltpu.VMEM((every, latents), F32),
            pltpu.VMEM((every, width), F32),
            pltpu.VMEM((PARTS * n, rows, width), BF16),
            pltpu.VMEM((PARTS * n, rows, width), BF16),
            pltpu.VMEM((PARTS * nb, thin, width), BF16),
            pltpu.VMEM((PARTS * nb, thin, width), BF16),
            pltpu.VMEM((PARTS * nb, thin, width), BF16),
            pltpu.VMEM((PARTS * nb, thin, width), BF16),
            pltpu.VMEM((PARTS * nb, width), F32),
            pltpu.VMEM((nb, 128), F32),
            pltpu.VMEM((nb, nb, 128), F32),
            pltpu.VMEM((nb, 128), F32),
            pltpu.VMEM((n, nb, 128), F32),
            sem((2,)), sem((4, PARTS, 2)),
            sem((PARTS, 2, steps)), sem((PARTS, 2, steps)),
            sem((PARTS, n)), sem((PARTS, n)),
            sem((PARTS, 2, steps)), sem((PARTS, 2, steps)),
            sem((PARTS, nb)), sem((PARTS, nb)),
            sem((PARTS, nb)), sem((PARTS, nb)),
            sem((nb,)), sem((nb,)),
            sem((n,)), sem((n,)),
            sem((PARTS, 2, steps)), sem((PARTS, 2, steps)),
        ],
        compiler_params=pltpu.CompilerParams(
            collective_id=0, has_side_effects=True, vmem_limit_bytes=60 * 1024 * 1024
        ),
    )(activations, activations.reshape(PARTS * nb, thin, width), encoder, encoder_bias.reshape(1, latents), decoder)
    encoder_grad = jnp.einsum("dr,rl->dl", gathered_t, pre_grads, preferred_element_type=F32).astype(BF16)
    decoder_grad = jnp.einsum("rl,rd->ld", active, upstream, preferred_element_type=F32).astype(BF16)
    return losses, encoder_grad, decoder_grad


def solution(mesh):
    n, nb = mesh.shape["shard"], mesh.shape["band"]
    return jax.shard_map(
        functools.partial(on_device, n, nb),
        mesh=mesh,
        in_specs=(
            P("shard", None),
            P(None, ("band", "shard")),
            P(("band", "shard")),
            P(("band", "shard"), None),
        ),
        out_specs=(P(), P(None, ("band", "shard")), P(("band", "shard"), None)),
        check_vma=False,
    )
```

```python
import functools

import jax
import jax.numpy as jnp
from jax import lax
from jax.experimental import pallas as pl
from jax.experimental.pallas import tpu as pltpu
from jax.sharding import PartitionSpec as P

MESH = pl.DeviceIdType.MESH
PARTS = 2
LAG = 0
F32 = jnp.float32
BF16 = jnp.bfloat16


def factors(count):
    outer = next(a for a in range(1, count + 1) if count % a == 0 and a * a >= count)
    return outer, count // outer


def ring_position(index, outer, inner):
    z, x = index // inner, index % inner
    return x * outer + z + (x % 2) * (outer - 1 - 2 * z)


def ring_index(position, outer, inner):
    x, r = position // outer, position % outer
    z = r + (x % 2) * (outer - 1 - 2 * r)
    return z * inner + x


def tile_of(extent, most):
    return next(t for t in range(most, 0, -128) if extent % t == 0)


def kernel(
    n, nb,
    act_ref, act3_ref, enc_hbm, bias_ref, dec_hbm,
    gath_t_hbm, ups_hbm, active_hbm, pregr_hbm, loss_ref,
    gath, gath_t, ups, active, pregr,
    enc, dec, linear, part, sendb, recvb, xsend, xrecv, usend, urecv, loss_acc, loss1s, loss1, loss2s, loss2,
    load_sem, out_sem,
    ag_s, ag_r, pt_s, pt_r, rs_s, rs_r, bx_s, bx_r, bu_s, bu_r, l1_s, l1_r, l2_s, l2_r, ug_s, ug_r,
):
    width = act_ref.shape[1]
    rows = act_ref.shape[0] // PARTS
    half = rows // 2
    thin = rows // nb
    fwd, bwd = n // 2, n // 2 - 1
    outer, inner = factors(n)
    band = lax.axis_index("band")
    shard = lax.axis_index("shard")
    core = band % 2
    sign = 1 - 2 * core
    place = ring_position(shard, outer, inner)
    nxt = {"shard": ring_index((place + n + sign) % n, outer, inner)}
    prv = {"shard": ring_index((place + n - sign) % n, outer, inner)}
    mate = {"band": band + sign}

    load_enc = pltpu.make_async_copy(enc_hbm, enc, load_sem.at[0])
    load_dec = pltpu.make_async_copy(dec_hbm, dec, load_sem.at[1])
    load_enc.start()
    load_dec.start()

    barrier = pltpu.get_barrier_semaphore()
    for device in [nxt, prv] + [{"band": (band + i) % nb} for i in range(1, nb)]:
        pl.semaphore_signal(barrier, inc=1, device_id=device, device_id_type=MESH)
    pl.semaphore_wait(barrier, nb + 1)

    started = []
    written = []

    def remote(src, dst, send, recv, device):
        return pltpu.make_async_remote_copy(
            src_ref=src, dst_ref=dst, send_sem=send, recv_sem=recv, device_id=device, device_id_type=MESH
        )

    def go(copy):
        copy.start()
        started.append(copy)
        return copy

    def write(src, dst, index):
        copy = pltpu.make_async_copy(src, dst, out_sem.at[index])
        copy.start()
        written.append(copy)

    tile = tile_of(width, 768)
    step_cols = tile_of(width, 256)
    l1 = []

    def batch(m):
        base = m * n * rows

        def at(slot):
            return pl.ds(base + slot * rows, rows)

        def group_span(upper):
            return pl.ds(base + upper * fwd * rows, fwd * rows)

        def held(slot):
            start = pl.multiple_of(base + slot * rows + core * half, half)
            return gath.at[pl.ds(start, half), :]

        mine = act_ref.at[pl.ds(pl.multiple_of(m * rows + core * half, half), half), :]

        def ag_copy(way, t):
            if way == 0:
                src = mine if t == 1 else held(n - t + 1)
                return remote(src, held(n - t), ag_s.at[m, 0, t], ag_r.at[m, 0, t], nxt)
            src = mine if t == 1 else held(t - 1)
            return remote(src, held(t), ag_s.at[m, 1, t], ag_r.at[m, 1, t], prv)

        def mate_copy(slot):
            there = n - slot
            return remote(held(slot), held(there), pt_s.at[m, slot], pt_r.at[m, there], mate)

        def mate_wait(s):
            remote(held(s), held(s), pt_s.at[m, n - s], pt_r.at[m, s], mate).wait_recv()

        def preact(upper):
            span = group_span(upper)
            value = jnp.dot(gath[span, :], enc[...], preferred_element_type=F32) + bias_ref[...]
            value = jnp.maximum(value, 0.0)
            linear[span, :] = value
            active[span, :] = (value * value).astype(BF16)
            write(active.at[span, :], active_hbm.at[span, :], (0, m, upper))

        def transpose(upper):
            span = group_span(upper)
            gath_t[:, span] = gath[span, :].T
            write(gath_t.at[:, span], gath_t_hbm.at[:, span], (1, m, upper))

        def decode(upper):
            span = group_span(upper)

            def body(i, carry):
                cols = pl.ds(pl.multiple_of(i * tile, tile), tile)
                part[span, cols] = jnp.dot(active[span, :], dec[:, cols], preferred_element_type=F32)
                return carry

            lax.fori_loop(0, width // tile, body, 0)

        ag = {(0, 1): go(ag_copy(0, 1)), (1, 1): go(ag_copy(1, 1))}
        gath[at(0), :] = act_ref[pl.ds(m * rows, rows), :]
        yield
        for t in range(1, fwd + 1):
            ag[0, t].wait_recv()
            if t < fwd:
                ag[0, t + 1] = go(ag_copy(0, t + 1))
            go(mate_copy(n - t))
            if t <= bwd:
                ag[1, t].wait_recv()
                if t < bwd:
                    ag[1, t + 1] = go(ag_copy(1, t + 1))
                go(mate_copy(t))
            if t < fwd:
                yield
            if t == bwd:
                for s in range(1, fwd):
                    mate_wait(s)
                if m == 0:
                    load_enc.wait()
                preact(0)
        for s in range(fwd, n):
            mate_wait(s)
        if bwd == 0:
            if m == 0:
                load_enc.wait()
            preact(0)
        preact(1)
        if m == 0:
            load_dec.wait()
        decode(1)

        rs = {}

        def rs_copy(way, t):
            slot = fwd - t + 1 if way == 0 else fwd + t
            there = slot - 1 if way == 0 else (slot + 1 if slot + 1 < n else fwd)
            return remote(
                sendb.at[m * n + slot], recvb.at[m * n + there], rs_s.at[m, way, t], rs_r.at[m, way, t],
                nxt if way == 0 else prv,
            )

        for t in range(1, fwd + 1):
            for way in (0, 1):
                if way == 1 and t > bwd:
                    continue
                slot = fwd - t + 1 if way == 0 else fwd + t
                value = part[at(slot), :]
                if t > 1:
                    rs[way, t - 1].wait_recv()
                    value = value + recvb[m * n + slot].astype(F32)
                sendb[m * n + slot] = value.astype(BF16)
                rs[way, t] = go(rs_copy(way, t))
            yield
            if t == 1:
                decode(0)
        if bwd:
            rs[1, bwd].wait_recv()
        rs[0, fwd].wait_recv()
        value = part[at(0), :] + recvb[m * n].astype(F32)
        if bwd:
            value = value + recvb[m * n + fwd].astype(F32)
        part[at(0), :] = value
        for k in range(nb):
            xsend[m * nb + k] = part[pl.ds(base + k * thin, thin), :].astype(BF16)
        bx = [
            go(remote(
                xsend.at[m * nb + (band + i) % nb], xrecv.at[m * nb + band], bx_s.at[m, i], bx_r.at[m, i],
                {"band": (band + i) % nb},
            ))
            for i in range(1, nb)
        ]
        xrecv[m * nb + band] = xsend[m * nb + band]
        transpose(0)
        yield
        for copy in bx:
            copy.wait_recv()

        def errors(i, carry):
            cols = pl.ds(pl.multiple_of(i * step_cols, step_cols), step_cols)
            left = act3_ref[m * nb + band, :, cols].astype(F32)
            all_errors = []
            for k in range(nb):
                left = left - xrecv[m * nb + k, :, cols].astype(F32)
                all_errors.append(left)
                loss_acc[pl.ds(m * nb + k, 1), cols] = jnp.sum(left * left, axis=0, keepdims=True)
            total = jnp.zeros_like(left)
            for k in reversed(range(nb)):
                total = total + all_errors[k]
                usend[m * nb + k, :, cols] = (-total / nb).astype(BF16)
            return carry

        lax.fori_loop(0, width // step_cols, errors, 0)
        bu = [
            go(remote(
                usend.at[m * nb + (band + i) % nb], urecv.at[m * nb + band], bu_s.at[m, i], bu_r.at[m, i],
                {"band": (band + i) % nb},
            ))
            for i in range(1, nb)
        ]
        urecv[m * nb + band] = usend[m * nb + band]
        if m == PARTS - 1:
            sums = loss_acc[pl.ds(0, nb), :]
            for other in range(1, PARTS):
                sums = sums + loss_acc[pl.ds(other * nb, nb), :]
            loss1s[...] = jnp.broadcast_to(jnp.sum(sums, axis=1, keepdims=True), loss1s.shape)
            for i in range(1, nb):
                l1.append(go(remote(
                    loss1s, loss1.at[i], l1_s.at[i], l1_r.at[i], {"band": (band + i) % nb}
                )))
        transpose(1)
        yield
        for copy in bu:
            copy.wait_recv()
        ups[at(0), :] = jnp.concatenate([urecv[m * nb + k].astype(F32) for k in range(nb)], axis=0).astype(BF16)

        def ug_copy(way, t):
            if way == 0:
                slot, there, device = (n - t + 1) % n, n - t, nxt
            else:
                slot, there, device = t - 1, t, prv
            return remote(ups.at[at(slot), :], ups.at[at(there), :], ug_s.at[m, way, t], ug_r.at[m, way, t], device)

        def backward(upper):
            span = group_span(upper)
            grads = lax.dot_general(ups[span, :], dec[...], (((1,), (1,)), ((), ())), preferred_element_type=F32)
            pregr[span, :] = (2.0 * linear[span, :] * grads).astype(BF16)
            write(pregr.at[span, :], pregr_hbm.at[span, :], (3, m, upper))

        ug = {}
        for way in (0, 1):
            if way == 0 or bwd:
                ug[way, 1] = go(ug_copy(way, 1))
        yield
        for t in range(1, fwd + 1):
            for way in (0, 1):
                last = fwd if way == 0 else bwd
                if t > last:
                    continue
                ug[way, t].wait_recv()
                if t < last:
                    ug[way, t + 1] = go(ug_copy(way, t + 1))
            if t == fwd:
                write(ups.at[group_span(1), :], ups_hbm.at[group_span(1), :], (2, m, 1))
            yield
            if t == max(bwd, 1):
                write(ups.at[group_span(0), :], ups_hbm.at[group_span(0), :], (2, m, 0))
                backward(0)
        backward(1)

    work = [batch(m) for m in range(PARTS)]
    done = set()
    turn = 0
    while len(done) < PARTS:
        for m in range(PARTS):
            if m in done or turn < m * LAG:
                continue
            if next(work[m], "end") == "end":
                done.add(m)
        turn += 1
        if not len(done) and l1 and turn == n + 4 + (PARTS - 1) * LAG:
            for copy in l1:
                copy.wait_recv()
            total = loss1s[...]
            for i in range(1, nb):
                total = total + loss1[i]
            loss2s[...] = total
            l2 = [
                go(remote(loss2s, loss2.at[i], l2_s.at[i], l2_r.at[i], {"shard": (shard + i) % n}))
                for i in range(1, n)
            ]
    for copy in l2:
        copy.wait_recv()
    total = loss2s[...]
    for i in range(1, n):
        total = total + loss2[i]
    for k in range(nb):
        loss_ref[k] = jnp.sum(total[k:k + 1, 0:1]) / (n * act_ref.shape[0] * width)
    for copy in started:
        copy.wait_send()
    for copy in written:
        copy.wait()


def on_device(n, nb, activations, encoder, encoder_bias, decoder):
    local, width = activations.shape
    latents = encoder.shape[1]
    rows = local // PARTS
    every = n * local
    thin = rows // nb
    sem = pltpu.SemaphoreType.DMA
    vmem = pl.BlockSpec(memory_space=pltpu.VMEM)
    hbm = pl.BlockSpec(memory_space=pl.ANY)
    steps = n // 2 + 1
    gathered_t, upstream, active, pre_grads, losses = pl.pallas_call(
        functools.partial(kernel, n, nb),
        out_shape=(
            jax.ShapeDtypeStruct((width, every), BF16),
            jax.ShapeDtypeStruct((every, width), BF16),
            jax.ShapeDtypeStruct((every, latents), BF16),
            jax.ShapeDtypeStruct((every, latents), BF16),
            jax.ShapeDtypeStruct((nb,), F32),
        ),
        in_specs=[vmem, vmem, hbm, vmem, hbm],
        out_specs=[hbm] * 4 + [pl.BlockSpec(memory_space=pltpu.SMEM)],
        scratch_shapes=[
            pltpu.VMEM((every, width), BF16),
            pltpu.VMEM((width, every), BF16),
            pltpu.VMEM((every, width), BF16),
            pltpu.VMEM((every, latents), BF16),
            pltpu.VMEM((every, latents), BF16),
            pltpu.VMEM((width, latents), BF16),
            pltpu.VMEM((latents, width), BF16),
            pltpu.VMEM((every, latents), F32),
            pltpu.VMEM((every, width), F32),
            pltpu.VMEM((PARTS * n, rows, width), BF16),
            pltpu.VMEM((PARTS * n, rows, width), BF16),
            pltpu.VMEM((PARTS * nb, thin, width), BF16),
            pltpu.VMEM((PARTS * nb, thin, width), BF16),
            pltpu.VMEM((PARTS * nb, thin, width), BF16),
            pltpu.VMEM((PARTS * nb, thin, width), BF16),
            pltpu.VMEM((PARTS * nb, width), F32),
            pltpu.VMEM((nb, 128), F32),
            pltpu.VMEM((nb, nb, 128), F32),
            pltpu.VMEM((nb, 128), F32),
            pltpu.VMEM((n, nb, 128), F32),
            sem((2,)), sem((4, PARTS, 2)),
            sem((PARTS, 2, steps)), sem((PARTS, 2, steps)),
            sem((PARTS, n)), sem((PARTS, n)),
            sem((PARTS, 2, steps)), sem((PARTS, 2, steps)),
            sem((PARTS, nb)), sem((PARTS, nb)),
            sem((PARTS, nb)), sem((PARTS, nb)),
            sem((nb,)), sem((nb,)),
            sem((n,)), sem((n,)),
            sem((PARTS, 2, steps)), sem((PARTS, 2, steps)),
        ],
        compiler_params=pltpu.CompilerParams(
            collective_id=0, has_side_effects=True, vmem_limit_bytes=60 * 1024 * 1024
        ),
    )(activations, activations.reshape(PARTS * nb, thin, width), encoder, encoder_bias.reshape(1, latents), decoder)
    def grads(e_ref, f_ref, g_ref, h_ref, eo_ref, do_ref):
        eo_ref[...] = jnp.dot(e_ref[...], f_ref[...], preferred_element_type=F32).astype(BF16)
        do_ref[...] = lax.dot_general(
            g_ref[...], h_ref[...], (((0,), (0,)), ((), ())), preferred_element_type=F32
        ).astype(BF16)

    wide = tile_of(width, 1152)
    encoder_grad, decoder_grad = pl.pallas_call(
        grads,
        grid=(width // wide,),
        out_shape=(
            jax.ShapeDtypeStruct((width, latents), BF16),
            jax.ShapeDtypeStruct((latents, width), BF16),
        ),
        in_specs=[
            pl.BlockSpec((wide, every), lambda i: (i, 0)),
            pl.BlockSpec((every, latents), lambda i: (0, 0)),
            pl.BlockSpec((every, latents), lambda i: (0, 0)),
            pl.BlockSpec((every, wide), lambda i: (0, i)),
        ],
        out_specs=[
            pl.BlockSpec((wide, latents), lambda i: (i, 0)),
            pl.BlockSpec((latents, wide), lambda i: (0, i)),
        ],
        compiler_params=pltpu.CompilerParams(vmem_limit_bytes=60 * 1024 * 1024),
    )(gathered_t, pre_grads, active, upstream)
    return losses, encoder_grad, decoder_grad


def solution(mesh):
    n, nb = mesh.shape["shard"], mesh.shape["band"]
    return jax.shard_map(
        functools.partial(on_device, n, nb),
        mesh=mesh,
        in_specs=(
            P("shard", None),
            P(None, ("band", "shard")),
            P(("band", "shard")),
            P(("band", "shard"), None),
        ),
        out_specs=(P(), P(None, ("band", "shard")), P(("band", "shard"), None)),
        check_vma=False,
    )
```
